256 devices in a mesh: scene: 16 (over x, y), space: 16 (over z, core).
Axes of the slice: x: 4, y: 4, z: 8, core: 2. Of those that a mesh axis runs over, the one named last changes fastest.
Arguments:
- queries: bfloat16 [196608, 1024], P(('scene', 'space')), parts along dimension 0
- keys: bfloat16 [196608, 1024], P(('scene', 'space')), parts along dimension 0
- values: bfloat16 [196608, 1024], P(('scene', 'space')), parts along dimension 0, may hold values from -6 to 6
- grad_out: bfloat16 [196608, 1024], P(('scene', 'space')), parts along dimension 0, may hold values from -6 to 6
- pattern: int32 [1536, 8], P('scene'), parts along dimension 0, may hold values from 0 to 95, as said below
- counts: int32 [1536], P('scene'), parts along dimension 0, may hold values from 64 to 128, as said below
Outputs:
- grad_queries: bfloat16 [196608, 1024], P(('scene', 'space')), parts along dimension 0
- grad_keys: bfloat16 [196608, 1024], P(('scene', 'space')), parts along dimension 0
- grad_values: bfloat16 [196608, 1024], P(('scene', 'space')), parts along dimension 0
The draws below stay inside these ranges and needn't reach their ends.
There are 16 independent parts, one for each index of `scene`. The reference program is written for one: setup_inputs(seed, part) draws one part's arguments, and reference() takes and returns one part's arrays. A program takes and returns all parts, laid end to end along the dimension named above; each array names one. Nothing has to cross between parts.
Inputs may be any that keep to these rules, and one draw needn't show every extreme that they name: `pattern`: slot 0 of row p is p itself; the other slots are distinct ids (p + o) mod 96 with 0 < |o| <= 6. `counts`: at least one patch is full.
All inputs are finite; a program needn't handle non-finite values.
Results may differ from the reference program's by a relative error of at most 0.0074.
Values may be sent and summed in bfloat16 or wider, within the bound.
A program may use at most 192 MiB of HBM per device.

```python
import math
import jax
import jax.numpy as jnp
from jax import lax

D = 1024
HEADS = 16
HEAD_DIM = 64
PATCH = 128
NB = 8
P_DEV = 6
PATCHES = 96
TOKENS = 12288


def final_keys(key):
    base_rows = jax.random.normal(jax.random.fold_in(key, 11), (PATCHES * PATCH, D), jnp.float32)
    return base_rows


def draw_keys(key, part):
    return final_keys(key).astype(jnp.bfloat16)


def draw_queries(key, part):
    base_rows = jax.random.normal(jax.random.fold_in(key, 19), (PATCHES * PATCH, D), jnp.float32)
    return base_rows.astype(jnp.bfloat16)


def draw_pattern(key, part):
    reach = P_DEV
    candidates = jnp.concatenate([jnp.arange(-reach, 0, dtype=jnp.int32), jnp.arange(1, reach + 1, dtype=jnp.int32)])
    raw_scores = jax.random.randint(jax.random.fold_in(key, 29), (PATCHES, 2 * reach), 0, 1 << 20)
    ranked = raw_scores * (2 * reach) + jnp.arange(2 * reach, dtype=jnp.int32)[None, :]
    order = jnp.argsort(ranked, axis=1, stable=True)[:, :NB - 1]
    offsets = candidates[order]
    own_ids = jnp.arange(PATCHES, dtype=jnp.int32)[:, None]
    others = (own_ids + offsets) % PATCHES
    return jnp.concatenate([own_ids, others], axis=1).astype(jnp.int32)


def draw_counts(key, part):
    raw_counts = jax.random.randint(jax.random.fold_in(key, 31), (PATCHES,), PATCH // 2, PATCH + 1)
    full_patch = jax.random.permutation(jax.random.fold_in(key, 37), PATCHES)[0]
    return raw_counts.at[full_patch].set(PATCH).astype(jnp.int32)


def levels(own_key, dims, shards, low, largest):
    level = 1.0
    for axis_at, blocks in shards:
        draws = jax.random.uniform(jax.random.fold_in(jax.random.fold_in(own_key, 6), axis_at), (blocks,), jnp.float32, low / len(shards), largest / len(shards))
        level = level * jnp.repeat(jnp.exp(draws), dims[axis_at] // blocks).reshape((-1,) + (1,) * (len(dims) - 1 - axis_at))
    return level


def centred(own_key, dims, deviation, limit, shards=(), kind=jnp.bfloat16):
    factor_of = levels(own_key, dims, shards, -0.22, 0.18) if shards else 1.0
    values = jax.random.normal(own_key, dims, jnp.float32) * deviation * factor_of
    return jnp.minimum(jnp.maximum(values, -limit), limit).astype(kind)


def setup_inputs(seed: int = 0, part: int = 0) -> dict:
    key_list = jax.random.split(jax.random.key(seed), 7)
    part_keys = jax.random.split(jax.random.fold_in(key_list[6], part), 7)
    return {
        "queries": draw_queries(jax.random.fold_in(jax.random.fold_in(key_list[6], part), 71), part),
        "keys": draw_keys(jax.random.fold_in(jax.random.fold_in(key_list[6], part), 71), part),
        "values": centred(part_keys[2], (TOKENS, D), 1.0, 6.0, ((0, 16),)),
        "grad_out": centred(part_keys[3], (TOKENS, D), 1.0, 6.0, ((0, 16),)),
        "pattern": draw_pattern(jax.random.fold_in(jax.random.fold_in(key_list[6], part), 71), part),
        "counts": draw_counts(jax.random.fold_in(jax.random.fold_in(key_list[6], part), 71), part),
    }


def patch_terms(query_rows, grad_rows, key_block, value_block, key_mask):
    scaling = 1.0 / math.sqrt(HEAD_DIM)
    query_heads = query_rows.astype(jnp.float32).reshape(PATCH, HEADS, HEAD_DIM)
    grad_heads = grad_rows.astype(jnp.float32).reshape(PATCH, HEADS, HEAD_DIM)
    key_heads = key_block.astype(jnp.float32).reshape(-1, HEADS, HEAD_DIM)
    value_heads = value_block.astype(jnp.float32).reshape(-1, HEADS, HEAD_DIM)
    scores = jnp.einsum('ihd,jhd->hij', query_heads, key_heads) * scaling
    masked = jnp.where(key_mask[None, None, :], scores, -jnp.inf)
    row_max = lax.optimization_barrier(jnp.max(masked, axis=-1, keepdims=True))
    weights = jnp.exp(masked - row_max)
    totals = lax.optimization_barrier(jnp.sum(weights, axis=-1, keepdims=True))
    attention = weights / totals
    attention_low = attention.astype(jnp.bfloat16).astype(jnp.float32)
    output_rows = jnp.einsum('hij,jhd->ihd', attention_low, value_heads)
    deltas = lax.optimization_barrier(jnp.sum(grad_heads * output_rows, axis=-1)).T
    grad_scores = jnp.einsum('ihd,jhd->hij', grad_heads, value_heads)
    score_grad = (attention * (grad_scores - deltas[:, :, None])).astype(jnp.bfloat16).astype(jnp.float32)
    grad_query = (jnp.einsum('hij,jhd->ihd', score_grad, key_heads) * scaling).reshape(PATCH, D).astype(jnp.bfloat16)
    grad_key = (jnp.einsum('hij,ihd->jhd', score_grad, query_heads) * scaling).reshape(-1, D)
    grad_value = jnp.einsum('hij,ihd->jhd', attention_low, grad_heads).reshape(-1, D)
    return (grad_query, grad_key, grad_value)

def reference(queries, keys, values, grad_out, pattern, counts):
    query_patches = queries.reshape(PATCHES, PATCH, D)
    grad_patches = grad_out.reshape(PATCHES, PATCH, D)
    key_patches = keys.reshape(PATCHES, PATCH, D)
    value_patches = values.reshape(PATCHES, PATCH, D)
    valid_rows = jnp.arange(PATCH, dtype=jnp.int32)[None, :] < counts[:, None]

    def step_patch(carry, patch_index):
        key_accum, value_accum = carry
        listed = pattern[patch_index]
        key_block = key_patches[listed].reshape(NB * PATCH, D)
        value_block = value_patches[listed].reshape(NB * PATCH, D)
        key_mask = valid_rows[listed].reshape(NB * PATCH)
        grad_query, grad_key, grad_value = patch_terms(query_patches[patch_index], grad_patches[patch_index], key_block, value_block, key_mask)
        key_accum = key_accum.at[listed].add(grad_key.reshape(NB, PATCH, D))
        value_accum = value_accum.at[listed].add(grad_value.reshape(NB, PATCH, D))
        return ((key_accum, value_accum), grad_query)
    zeros_start = jnp.zeros((PATCHES, PATCH, D), jnp.float32)
    (key_accum, value_accum), grad_rows = lax.scan(step_patch, (zeros_start, zeros_start), jnp.arange(PATCHES, dtype=jnp.int32))
    grad_queries = grad_rows.reshape(TOKENS, D)
    grad_keys = key_accum.reshape(TOKENS, D).astype(jnp.bfloat16)
    grad_values = value_accum.reshape(TOKENS, D).astype(jnp.bfloat16)
    return (grad_queries, grad_keys, grad_values)
```

```python
import functools

import jax
import jax.numpy as jnp
from jax import lax
from jax.experimental import pallas as pl
from jax.experimental.pallas import tpu as pltpu
from jax.sharding import PartitionSpec as P

HEADS = 16
PATCH = 128
LANES = 128
AHEAD = 3
LAG = 2


def nt(a, b):
    return lax.dot_general(a, b, (((1,), (1,)), ((), ())), preferred_element_type=jnp.float32)


def nn(a, b):
    return lax.dot_general(a, b, (((1,), (0,)), ((), ())), preferred_element_type=jnp.float32)


def kernel(
    devices,
    per,
    listed,
    total,
    pat,
    cnt,
    q_hbm,
    k_hbm,
    v_hbm,
    do_hbm,
    dq_hbm,
    dk_hbm,
    dv_hbm,
    kext,
    vext,
    qin,
    doin,
    kcur,
    vcur,
    ktb,
    qb,
    dob,
    sb,
    dpb,
    pb,
    dsb,
    ck,
    cv,
    gsend,
    grecv,
    own,
    dqs,
    dks,
    dvs,
    lid,
    inv,
    ecnt,
    loc_sem,
    kv_ssem,
    kv_rsem,
    gr_ssem,
    gr_rsem,
    out_sem,
):
    groups = kext.shape[0]
    ext = 3 * per
    me = lax.axis_index("space")
    right = lax.rem(me + 1, devices)
    left = lax.rem(me + devices - 1, devices)

    def cols(g):
        return pl.ds(pl.multiple_of(g * LANES, LANES), LANES)

    def local(which, g):
        src = (k_hbm, v_hbm, q_hbm, do_hbm)[which].at[:, :, cols(g)]
        dst = (
            kext.at[g, pl.ds(per, per)],
            vext.at[g, pl.ds(per, per)],
            qin.at[g],
            doin.at[g],
        )[which]
        return pltpu.make_async_copy(src, dst, loc_sem.at[which, g])

    def kv_send(which, g):
        src = (k_hbm, v_hbm)[which // 2].at[:, :, cols(g)]
        buf = (kext, vext)[which // 2]
        low = 0 if which % 2 == 0 else 2 * per
        return pltpu.make_async_remote_copy(
            src_ref=src,
            dst_ref=buf.at[g, pl.ds(low, per)],
            send_sem=kv_ssem.at[which, g],
            recv_sem=kv_rsem.at[which, g],
            device_id={"space": right if which % 2 == 0 else left},
            device_id_type=pl.DeviceIdType.MESH,
        )

    def gr_send(which, g):
        return pltpu.make_async_remote_copy(
            src_ref=gsend.at[g, which],
            dst_ref=grecv.at[g, which],
            send_sem=gr_ssem.at[which, g],
            recv_sem=gr_rsem.at[which, g],
            device_id={"space": left if which % 2 == 0 else right},
            device_id_type=pl.DeviceIdType.MESH,
        )

    def out(which, g):
        src = (dqs, dks, dvs)[which].at[g]
        dst = (dq_hbm, dk_hbm, dv_hbm)[which].at[:, :, cols(g)]
        return pltpu.make_async_copy(src, dst, out_sem.at[which, g])

    @pl.loop(0, groups)
    def _(g):
        for which in range(4):
            local(which, g).start()

    barrier = pltpu.get_barrier_semaphore()
    for neighbour in (left, right):
        pl.semaphore_signal(
            barrier, inc=1, device_id={"space": neighbour}, device_id_type=pl.DeviceIdType.MESH
        )
    pl.semaphore_wait(barrier, 2)

    @pl.loop(0, AHEAD)
    def _(g):
        for which in range(4):
            kv_send(which, g).start()

    base = me * per - per

    def wrap(x):
        x = jnp.where(x < 0, x + total, x)
        return jnp.where(x >= total, x - total, x)

    for t in range(ext):
        ecnt[t] = cnt[wrap(base + t)]
    for i in range(per):
        ids = [jnp.clip(wrap(pat[me * per + i, j] - base), 0, ext - 1) for j in range(listed)]
        for j in range(listed):
            lid[i, j] = ids[j]
        for o in range(2 * per + 1):
            slot = jnp.int32(listed)
            for j in range(listed):
                slot = jnp.where(ids[j] == i + o, j, slot)
            inv[i, o] = slot
        ck[i, listed] = jnp.zeros((PATCH, LANES), jnp.float32)
        cv[i, listed] = jnp.zeros((PATCH, LANES), jnp.float32)

    lane_low = lax.broadcasted_iota(jnp.int32, (PATCH, LANES), 1) < LANES // 2
    row_low = lax.broadcasted_iota(jnp.int32, (LANES, PATCH), 0) < LANES // 2
    half_row = lax.broadcasted_iota(jnp.int32, (PATCH // 2, 2 * PATCH), 0) + PATCH // 2

    def finish(g):
        for which in range(4):
            gr_send(which, g).wait_recv()
        for kind, stage in ((0, dks), (1, dvs)):

            @pl.loop(0, per)
            def _(p):
                stage[g, p] = (
                    own[g, kind, p]
                    + grecv[g, 2 * kind, p].astype(jnp.float32)
                    + grecv[g, 2 * kind + 1, p].astype(jnp.float32)
                ).astype(jnp.bfloat16)

        out(1, g).start()
        out(2, g).start()

    @pl.loop(0, groups)
    def _(g):
        @pl.when(g + AHEAD < groups)
        def _():
            for which in range(4):
                kv_send(which, g + AHEAD).start()

        for which in range(4):
            local(which, g).wait()
        for which in range(4):
            kv_send(which, g).wait_recv()

        @pl.loop(0, ext)
        def _(t):
            k = kext[g, t]
            kcur[t] = k
            vcur[t] = vext[g, t]
            ktb[t] = k.T

        sides = {}
        tops = {}

        def products(i):
            q = qin[g, i] * jnp.bfloat16(0.125)
            do = doin[g, i]
            zero = jnp.zeros_like(q)
            qd = jnp.concatenate([jnp.where(lane_low, q, zero), jnp.where(lane_low, zero, q)], 0)
            dd = jnp.concatenate([jnp.where(lane_low, do, zero), jnp.where(lane_low, zero, do)], 0)
            qb[i % 3][...] = qd
            dob[i % 3][...] = dd
            ids = [lid[i, j] for j in range(listed)]
            s = nt(jnp.concatenate([kcur[t] for t in ids], 0), qd)
            top = None
            for j in range(listed):
                low, high = j * PATCH, j * PATCH + PATCH // 2
                s_low = s[low:high]
                s_high = jnp.where(half_row < ecnt[ids[j]], s[high : low + PATCH], -jnp.inf)
                sb[i % 2][low:high] = s_low
                sb[i % 2][high : low + PATCH] = s_high
                for part in (s_low, s_high):
                    part = jnp.max(part.reshape(-1, 8, 2 * PATCH), axis=0)
                    top = part if top is None else jnp.maximum(top, part)
            tops[i] = jnp.max(top, axis=0, keepdims=True)
            dpb[i % 2][...] = nt(jnp.concatenate([vcur[t] for t in ids], 0), dd)

        def middle(i):
            scores, grads = sb[i % 2], dpb[i % 2]
            top = tops[i]
            step = PATCH // 2
            total_e = total_d = None
            for low in range(0, listed * PATCH, step):
                e = jnp.exp(scores[low : low + step] - top)
                scores[low : low + step] = e
                d = e * grads[low : low + step]
                e = jnp.sum(e.reshape(-1, 8, 2 * PATCH), axis=0)
                d = jnp.sum(d.reshape(-1, 8, 2 * PATCH), axis=0)
                total_e = e if total_e is None else total_e + e
                total_d = d if total_d is None else total_d + d
            inverse = 1.0 / jnp.sum(total_e, axis=0, keepdims=True)
            delta = jnp.sum(total_d, axis=0, keepdims=True) * inverse
            for low in range(0, listed * PATCH, step):
                a = scores[low : low + step] * inverse
                pb[i % 2][low : low + step] = a.astype(jnp.bfloat16)
                dsb[i % 2][low : low + step] = (a * (grads[low : low + step] - delta)).astype(
                    jnp.bfloat16
                )

        def results(i):
            ds = dsb[i % 2][...]
            kt = jnp.concatenate([ktb[lid[i, j]] for j in range(listed)], 1)
            dq = nn(kt, ds)
            dq = jnp.where(row_low, dq[:, :PATCH], dq[:, PATCH:])
            dqs[g, i] = (dq.T * 0.125).astype(jnp.bfloat16)
            dk = nn(ds, qb[i % 3][...])
            dv = nn(pb[i % 2][...], dob[i % 3][...])
            for j in range(listed):
                ck[i, j] = dk[j * PATCH : (j + 1) * PATCH]
                cv[i, j] = dv[j * PATCH : (j + 1) * PATCH]

        for n in range(per + 2):
            if n >= 2:
                results(n - 2)
            if n < per:
                products(n)
            if 1 <= n <= per:
                middle(n - 1)

        out(0, g).start()

        for t in list(range(per)) + list(range(2 * per, ext)) + list(range(per, 2 * per)):
            first, last = max(0, t - 2 * per), min(per - 1, t)
            slots = [inv[i, t - i] for i in range(first, last + 1)]
            for kind, terms in ((0, ck), (1, cv)):
                value = functools.reduce(
                    jnp.add, [terms[i, slot] for i, slot in zip(range(first, last + 1), slots)]
                )
                if t < per:
                    gsend[g, 2 * kind, t] = value.astype(jnp.bfloat16)
                elif t >= 2 * per:
                    gsend[g, 2 * kind + 1, t - 2 * per] = value.astype(jnp.bfloat16)
                else:
                    own[g, kind, t - per] = value
        for which in range(4):
            gr_send(which, g).start()

        @pl.when(g >= LAG)
        def _():
            finish(g - LAG)

    @pl.loop(groups - LAG, groups)
    def _(g):
        finish(g)

    @pl.loop(0, groups)
    def _(g):
        for which in range(4):
            kv_send(which, g).wait_send()
            gr_send(which, g).wait_send()
        for which in range(3):
            out(which, g).wait()


def on_device(queries, keys, values, grad_out, pattern, counts):
    rows, width = queries.shape
    per = rows // PATCH
    total, listed = pattern.shape
    devices = lax.axis_size("space")
    groups = width // LANES
    ext = 3 * per
    shape = jax.ShapeDtypeStruct((per, PATCH, width), jnp.bfloat16)
    low = jnp.bfloat16
    full = jnp.float32
    anywhere = pl.BlockSpec(memory_space=pl.ANY)
    small = pl.BlockSpec(memory_space=pltpu.SMEM)
    outs = pl.pallas_call(
        functools.partial(kernel, devices, per, listed, total),
        out_shape=(shape,) * 3,
        in_specs=[small, small] + [anywhere] * 4,
        out_specs=[anywhere] * 3,
        scratch_shapes=[
            pltpu.VMEM((groups, ext, PATCH, LANES), low),
            pltpu.VMEM((groups, ext, PATCH, LANES), low),
            pltpu.VMEM((groups, per, PATCH, LANES), low),
            pltpu.VMEM((groups, per, PATCH, LANES), low),
            pltpu.VMEM((ext, PATCH, LANES), low),
            pltpu.VMEM((ext, PATCH, LANES), low),
            pltpu.VMEM((ext, LANES, PATCH), low),
            [pltpu.VMEM((2 * PATCH, LANES), low)] * 3,
            [pltpu.VMEM((2 * PATCH, LANES), low)] * 3,
            [pltpu.VMEM((listed * PATCH, 2 * PATCH), full)] * 2,
            [pltpu.VMEM((listed * PATCH, 2 * PATCH), full)] * 2,
            [pltpu.VMEM((listed * PATCH, 2 * PATCH), low)] * 2,
            [pltpu.VMEM((listed * PATCH, 2 * PATCH), low)] * 2,
            pltpu.VMEM((per, listed + 1, PATCH, LANES), full),
            pltpu.VMEM((per, listed + 1, PATCH, LANES), full),
            pltpu.VMEM((groups, 4, per, PATCH, LANES), low),
            pltpu.VMEM((groups, 4, per, PATCH, LANES), low),
            pltpu.VMEM((groups, 2, per, PATCH, LANES), full),
            pltpu.VMEM((groups, per, PATCH, LANES), low),
            pltpu.VMEM((groups, per, PATCH, LANES), low),
            pltpu.VMEM((groups, per, PATCH, LANES), low),
            pltpu.SMEM((per, listed), jnp.int32),
            pltpu.SMEM((per, 2 * per + 1), jnp.int32),
            pltpu.SMEM((ext,), jnp.int32),
            pltpu.SemaphoreType.DMA((4, groups)),
            pltpu.SemaphoreType.DMA((4, groups)),
            pltpu.SemaphoreType.DMA((4, groups)),
            pltpu.SemaphoreType.DMA((4, groups)),
            pltpu.SemaphoreType.DMA((4, groups)),
            pltpu.SemaphoreType.DMA((3, groups)),
        ],
        compiler_params=pltpu.CompilerParams(
            collective_id=0, has_side_effects=True, vmem_limit_bytes=60 * 1024 * 1024
        ),
        name="sparse_attention_backward",
    )(pattern, counts, *(x.reshape(per, PATCH, width) for x in (queries, keys, values, grad_out)))
    return tuple(x.reshape(rows, width) for x in outs)


def solution(mesh):
    rows = P(("scene", "space"), None)
    return jax.shard_map(
        on_device,
        mesh=mesh,
        in_specs=(rows, rows, rows, rows, P("scene", None), P("scene")),
        out_specs=(rows, rows, rows),
        check_vma=False,
    )
```

```python
import functools

import jax
import jax.numpy as jnp
from jax import lax
from jax.experimental import pallas as pl
from jax.experimental.pallas import tpu as pltpu
from jax.sharding import PartitionSpec as P

HEADS = 16
PATCH = 128
LANES = 128
AHEAD = 3
LAG = 2


def nt(a, b):
    return lax.dot_general(a, b, (((1,), (1,)), ((), ())), preferred_element_type=jnp.float32)


def nn(a, b):
    return lax.dot_general(a, b, (((1,), (0,)), ((), ())), preferred_element_type=jnp.float32)


def kernel(
    devices,
    per,
    listed,
    total,
    pat,
    cnt,
    q_hbm,
    k_hbm,
    v_hbm,
    do_hbm,
    dq_hbm,
    dk_hbm,
    dv_hbm,
    kvx,
    qin,
    doin,
    kcur,
    vcur,
    ktb,
    qb,
    dob,
    sb,
    dpb,
    pb,
    dsb,
    ck,
    cv,
    gsend,
    grecv,
    own,
    dqs,
    dks,
    dvs,
    lid,
    inv,
    ecnt,
    loc_sem,
    kv_ssem,
    kv_rsem,
    gr_ssem,
    gr_rsem,
    out_sem,
):
    groups = kvx.shape[0]
    ext = 3 * per
    me = lax.axis_index("space")
    right = lax.rem(me + 1, devices)
    left = lax.rem(me + devices - 1, devices)

    def cols(g):
        return pl.ds(pl.multiple_of(g * LANES, LANES), LANES)

    def local(which, g):
        src = (k_hbm, v_hbm, q_hbm, do_hbm)[which].at[:, :, cols(g)]
        dst = (kvx.at[g, 1, 0], kvx.at[g, 1, 1], qin.at[g], doin.at[g])[which]
        return pltpu.make_async_copy(src, dst, loc_sem.at[which, g])

    def kv_send(which, g):
        return pltpu.make_async_remote_copy(
            src_ref=kvx.at[g, 1],
            dst_ref=kvx.at[g, 2 * which],
            send_sem=kv_ssem.at[which, g],
            recv_sem=kv_rsem.at[which, g],
            device_id={"space": left if which else right},
            device_id_type=pl.DeviceIdType.MESH,
        )

    def gr_send(which, g):
        return pltpu.make_async_remote_copy(
            src_ref=gsend.at[g, which],
            dst_ref=grecv.at[g, which],
            send_sem=gr_ssem.at[which, g],
            recv_sem=gr_rsem.at[which, g],
            device_id={"space": right if which else left},
            device_id_type=pl.DeviceIdType.MESH,
        )

    def start_send(g):
        for which in range(2):
            local(which, g).wait()
        for which in range(2):
            kv_send(which, g).start()

    def out(which, g):
        src = (dqs, dks, dvs)[which].at[g]
        dst = (dq_hbm, dk_hbm, dv_hbm)[which].at[:, :, cols(g)]
        return pltpu.make_async_copy(src, dst, out_sem.at[which, g])

    @pl.loop(0, groups)
    def _(g):
        for which in range(4):
            local(which, g).start()

    barrier = pltpu.get_barrier_semaphore()
    for neighbour in (left, right):
        pl.semaphore_signal(
            barrier, inc=1, device_id={"space": neighbour}, device_id_type=pl.DeviceIdType.MESH
        )
    pl.semaphore_wait(barrier, 2)

    @pl.loop(0, AHEAD)
    def _(g):
        start_send(g)

    base = me * per - per

    def wrap(x):
        x = jnp.where(x < 0, x + total, x)
        return jnp.where(x >= total, x - total, x)

    for t in range(ext):
        ecnt[t] = cnt[wrap(base + t)]
    for i in range(per):
        ids = [jnp.clip(wrap(pat[me * per + i, j] - base), 0, ext - 1) for j in range(listed)]
        for j in range(listed):
            lid[i, j] = ids[j]
        for o in range(2 * per + 1):
            slot = jnp.int32(listed)
            for j in range(listed):
                slot = jnp.where(ids[j] == i + o, j, slot)
            inv[i, o] = slot
        ck[i, listed] = jnp.zeros((PATCH, LANES), jnp.float32)
        cv[i, listed] = jnp.zeros((PATCH, LANES), jnp.float32)

    lane_low = lax.broadcasted_iota(jnp.int32, (PATCH, LANES), 1) < LANES // 2
    row_low = lax.broadcasted_iota(jnp.int32, (LANES, PATCH), 0) < LANES // 2
    half_row = lax.broadcasted_iota(jnp.int32, (PATCH // 2, 2 * PATCH), 0) + PATCH // 2

    def finish(g):
        for which in range(2):
            gr_send(which, g).wait_recv()
        for kind, stage in ((0, dks), (1, dvs)):

            @pl.loop(0, per)
            def _(p):
                stage[g, p] = (
                    own[g, kind, p]
                    + grecv[g, 0, kind, p].astype(jnp.float32)
                    + grecv[g, 1, kind, p].astype(jnp.float32)
                ).astype(jnp.bfloat16)

        out(1, g).start()
        out(2, g).start()

    @pl.loop(0, groups)
    def _(g):
        @pl.when(g + AHEAD < groups)
        def _():
            start_send(g + AHEAD)

        for which in range(2, 4):
            local(which, g).wait()
        for which in range(2):
            kv_send(which, g).wait_recv()

        for side in range(3):

            @pl.loop(0, per)
            def _(p):
                k = kvx[g, side, 0, p]
                kcur[side * per + p] = k
                vcur[side * per + p] = kvx[g, side, 1, p]
                ktb[side * per + p] = k.T

        sides = {}
        tops = {}

        def products(i):
            q = qin[g, i] * jnp.bfloat16(0.125)
            do = doin[g, i]
            zero = jnp.zeros_like(q)
            qd = jnp.concatenate([jnp.where(lane_low, q, zero), jnp.where(lane_low, zero, q)], 0)
            dd = jnp.concatenate([jnp.where(lane_low, do, zero), jnp.where(lane_low, zero, do)], 0)
            qb[i % 3][...] = qd
            dob[i % 3][...] = dd
            ids = [lid[i, j] for j in range(listed)]
            s = nt(jnp.concatenate([kcur[t] for t in ids], 0), qd)
            top = None
            for j in range(listed):
                low, high = j * PATCH, j * PATCH + PATCH // 2
                s_low = s[low:high]
                s_high = jnp.where(half_row < ecnt[ids[j]], s[high : low + PATCH], -jnp.inf)
                sb[i % 2][low:high] = s_low
                sb[i % 2][high : low + PATCH] = s_high
                for part in (s_low, s_high):
                    part = jnp.max(part.reshape(-1, 8, 2 * PATCH), axis=0)
                    top = part if top is None else jnp.maximum(top, part)
            tops[i] = jnp.max(top, axis=0, keepdims=True)
            dpb[i % 2][...] = nt(jnp.concatenate([vcur[t] for t in ids], 0), dd)

        def middle(i):
            scores, grads = sb[i % 2], dpb[i % 2]
            top = tops[i]
            step = PATCH // 2
            total_e = total_d = None
            for low in range(0, listed * PATCH, step):
                e = jnp.exp(scores[low : low + step] - top)
                scores[low : low + step] = e
                d = e * grads[low : low + step]
                e = jnp.sum(e.reshape(-1, 8, 2 * PATCH), axis=0)
                d = jnp.sum(d.reshape(-1, 8, 2 * PATCH), axis=0)
                total_e = e if total_e is None else total_e + e
                total_d = d if total_d is None else total_d + d
            inverse = 1.0 / jnp.sum(total_e, axis=0, keepdims=True)
            delta = jnp.sum(total_d, axis=0, keepdims=True) * inverse
            for low in range(0, listed * PATCH, step):
                a = scores[low : low + step] * inverse
                pb[i % 2][low : low + step] = a.astype(jnp.bfloat16)
                dsb[i % 2][low : low + step] = (a * (grads[low : low + step] - delta)).astype(
                    jnp.bfloat16
                )

        def results(i):
            ds = dsb[i % 2][...]
            kt = jnp.concatenate([ktb[lid[i, j]] for j in range(listed)], 1)
            dq = nn(kt, ds)
            dq = jnp.where(row_low, dq[:, :PATCH], dq[:, PATCH:])
            dqs[g, i] = (dq.T * 0.125).astype(jnp.bfloat16)
            dk = nn(ds, qb[i % 3][...])
            dv = nn(pb[i % 2][...], dob[i % 3][...])
            for j in range(listed):
                ck[i, j] = dk[j * PATCH : (j + 1) * PATCH]
                cv[i, j] = dv[j * PATCH : (j + 1) * PATCH]

        for n in range(per + 2):
            if n >= 2:
                results(n - 2)
            if n < per:
                products(n)
            if 1 <= n <= per:
                middle(n - 1)

        out(0, g).start()

        for t in list(range(per)) + list(range(2 * per, ext)) + list(range(per, 2 * per)):
            first, last = max(0, t - 2 * per), min(per - 1, t)
            slots = [inv[i, t - i] for i in range(first, last + 1)]
            for kind, terms in ((0, ck), (1, cv)):
                value = functools.reduce(
                    jnp.add, [terms[i, slot] for i, slot in zip(range(first, last + 1), slots)]
                )
                if t < per:
                    gsend[g, 0, kind, t] = value.astype(jnp.bfloat16)
                elif t >= 2 * per:
                    gsend[g, 1, kind, t - 2 * per] = value.astype(jnp.bfloat16)
                else:
                    own[g, kind, t - per] = value
        for which in range(2):
            gr_send(which, g).start()

        @pl.when(g >= LAG)
        def _():
            finish(g - LAG)

    @pl.loop(groups - LAG, groups)
    def _(g):
        finish(g)

    @pl.loop(0, groups)
    def _(g):
        for which in range(2):
            kv_send(which, g).wait_send()
            gr_send(which, g).wait_send()
        for which in range(3):
            out(which, g).wait()


def on_device(queries, keys, values, grad_out, pattern, counts):
    rows, width = queries.shape
    per = rows // PATCH
    total, listed = pattern.shape
    devices = lax.axis_size("space")
    groups = width // LANES
    ext = 3 * per
    shape = jax.ShapeDtypeStruct((per, PATCH, width), jnp.bfloat16)
    low = jnp.bfloat16
    full = jnp.float32
    anywhere = pl.BlockSpec(memory_space=pl.ANY)
    small = pl.BlockSpec(memory_space=pltpu.SMEM)
    outs = pl.pallas_call(
        functools.partial(kernel, devices, per, listed, total),
        out_shape=(shape,) * 3,
        in_specs=[small, small] + [anywhere] * 4,
        out_specs=[anywhere] * 3,
        scratch_shapes=[
            pltpu.VMEM((groups, 3, 2, per, PATCH, LANES), low),
            pltpu.VMEM((groups, per, PATCH, LANES), low),
            pltpu.VMEM((groups, per, PATCH, LANES), low),
            pltpu.VMEM((ext, PATCH, LANES), low),
            pltpu.VMEM((ext, PATCH, LANES), low),
            pltpu.VMEM((ext, LANES, PATCH), low),
            [pltpu.VMEM((2 * PATCH, LANES), low)] * 3,
            [pltpu.VMEM((2 * PATCH, LANES), low)] * 3,
            [pltpu.VMEM((listed * PATCH, 2 * PATCH), full)] * 2,
            [pltpu.VMEM((listed * PATCH, 2 * PATCH), full)] * 2,
            [pltpu.VMEM((listed * PATCH, 2 * PATCH), low)] * 2,
            [pltpu.VMEM((listed * PATCH, 2 * PATCH), low)] * 2,
            pltpu.VMEM((per, listed + 1, PATCH, LANES), full),
            pltpu.VMEM((per, listed + 1, PATCH, LANES), full),
            pltpu.VMEM((groups, 2, 2, per, PATCH, LANES), low),
            pltpu.VMEM((groups, 2, 2, per, PATCH, LANES), low),
            pltpu.VMEM((groups, 2, per, PATCH, LANES), full),
            pltpu.VMEM((groups, per, PATCH, LANES), low),
            pltpu.VMEM((groups, per, PATCH, LANES), low),
            pltpu.VMEM((groups, per, PATCH, LANES), low),
            pltpu.SMEM((per, listed), jnp.int32),
            pltpu.SMEM((per, 2 * per + 1), jnp.int32),
            pltpu.SMEM((ext,), jnp.int32),
            pltpu.SemaphoreType.DMA((4, groups)),
            pltpu.SemaphoreType.DMA((2, groups)),
            pltpu.SemaphoreType.DMA((2, groups)),
            pltpu.SemaphoreType.DMA((2, groups)),
            pltpu.SemaphoreType.DMA((2, groups)),
            pltpu.SemaphoreType.DMA((3, groups)),
        ],
        compiler_params=pltpu.CompilerParams(
            collective_id=0, has_side_effects=True, vmem_limit_bytes=60 * 1024 * 1024
        ),
        name="sparse_attention_backward",
    )(pattern, counts, *(x.reshape(per, PATCH, width) for x in (queries, keys, values, grad_out)))
    return tuple(x.reshape(rows, width) for x in outs)


def solution(mesh):
    rows = P(("scene", "space"), None)
    return jax.shard_map(
        on_device,
        mesh=mesh,
        in_specs=(rows, rows, rows, rows, P("scene", None), P("scene")),
        out_specs=(rows, rows, rows),
        check_vma=False,
    )
```

```python
import functools

import jax
import jax.numpy as jnp
from jax import lax
from jax.experimental import pallas as pl
from jax.experimental.pallas import tpu as pltpu
from jax.sharding import PartitionSpec as P

HEADS = 16
PATCH = 128
LANES = 128
AHEAD = 3
LAG = 2
STEPS = 4


def nt(a, b):
    return lax.dot_general(a, b, (((1,), (1,)), ((), ())), preferred_element_type=jnp.float32)


def nn(a, b):
    return lax.dot_general(a, b, (((1,), (0,)), ((), ())), preferred_element_type=jnp.float32)


def kernel(
    devices,
    per,
    listed,
    total,
    pat,
    cnt,
    q_hbm,
    k_hbm,
    v_hbm,
    do_hbm,
    dq_hbm,
    dk_hbm,
    dv_hbm,
    kvx,
    qin,
    doin,
    kcur,
    vcur,
    ktb,
    qb,
    dob,
    sb,
    dpb,
    pb,
    dsb,
    ck,
    cv,
    gsend,
    grecv,
    own,
    dqs,
    dks,
    dvs,
    lid,
    inv,
    ecnt,
    loc_sem,
    kv_ssem,
    kv_rsem,
    gr_ssem,
    gr_rsem,
    out_sem,
):
    groups = kvx.shape[0]
    ext = 3 * per
    me = lax.axis_index("space")
    right = lax.rem(me + 1, devices)
    left = lax.rem(me + devices - 1, devices)

    def cols(g):
        return pl.ds(pl.multiple_of(g * LANES, LANES), LANES)

    def local(which, g):
        src = (k_hbm, v_hbm, q_hbm, do_hbm)[which].at[:, :, cols(g)]
        dst = (kvx.at[g, 1, 0], kvx.at[g, 1, 1], qin.at[g], doin.at[g])[which]
        return pltpu.make_async_copy(src, dst, loc_sem.at[which, g])

    def kv_send(which, g):
        return pltpu.make_async_remote_copy(
            src_ref=kvx.at[g, 1],
            dst_ref=kvx.at[g, 2 * which],
            send_sem=kv_ssem.at[which, g],
            recv_sem=kv_rsem.at[which, g],
            device_id={"space": left if which else right},
            device_id_type=pl.DeviceIdType.MESH,
        )

    def gr_send(which, g):
        return pltpu.make_async_remote_copy(
            src_ref=gsend.at[g, which],
            dst_ref=grecv.at[g, which],
            send_sem=gr_ssem.at[which, g],
            recv_sem=gr_rsem.at[which, g],
            device_id={"space": right if which else left},
            device_id_type=pl.DeviceIdType.MESH,
        )

    def start_send(g):
        for which in range(2):
            local(which, g).wait()
        for which in range(2):
            kv_send(which, g).start()

    def out(which, g):
        src = (dqs, dks, dvs)[which].at[g]
        dst = (dq_hbm, dk_hbm, dv_hbm)[which].at[:, :, cols(g)]
        return pltpu.make_async_copy(src, dst, out_sem.at[which, g])

    @pl.loop(0, groups)
    def _(g):
        for which in range(4):
            local(which, g).start()

    barrier = pltpu.get_barrier_semaphore()
    for neighbour in (left, right):
        pl.semaphore_signal(
            barrier, inc=1, device_id={"space": neighbour}, device_id_type=pl.DeviceIdType.MESH
        )
    pl.semaphore_wait(barrier, 2)

    @pl.loop(0, AHEAD)
    def _(g):
        start_send(g)

    base = me * per - per

    def wrap(x):
        x = jnp.where(x < 0, x + total, x)
        return jnp.where(x >= total, x - total, x)

    for t in range(ext):
        ecnt[t] = cnt[wrap(base + t)]
    for i in range(per):
        ids = [jnp.clip(wrap(pat[j, me * per + i] - base), 0, ext - 1) for j in range(listed)]
        for j in range(listed):
            lid[i, j] = ids[j]
        for o in range(2 * per + 1):
            slot = jnp.int32(listed)
            for j in range(listed):
                slot = jnp.where(ids[j] == i + o, j, slot)
            inv[i, o] = slot
        ck[i, listed] = jnp.zeros((PATCH, LANES), jnp.float32)
        cv[i, listed] = jnp.zeros((PATCH, LANES), jnp.float32)

    lane_low = lax.broadcasted_iota(jnp.int32, (PATCH, LANES), 1) < LANES // 2
    row_low = lax.broadcasted_iota(jnp.int32, (LANES, PATCH), 0) < LANES // 2
    half_row = lax.broadcasted_iota(jnp.int32, (PATCH // 2, 2 * PATCH), 0) + PATCH // 2

    def finish(g):
        for which in range(2):
            gr_send(which, g).wait_recv()
        for kind, stage in ((0, dks), (1, dvs)):

            @pl.loop(0, per)
            def _(p):
                stage[g, p] = (
                    own[g, kind, p]
                    + grecv[g, 0, kind, p].astype(jnp.float32)
                    + grecv[g, 1, kind, p].astype(jnp.float32)
                ).astype(jnp.bfloat16)

        out(1, g).start()
        out(2, g).start()

    @pl.loop(0, groups)
    def _(g):
        @pl.when(g + AHEAD < groups)
        def _():
            start_send(g + AHEAD)

        for which in range(2, 4):
            local(which, g).wait()
        for which in range(2):
            kv_send(which, g).wait_recv()

        for side in range(3):

            @pl.loop(0, per)
            def _(p):
                k = kvx[g, side, 0, p]
                kcur[side * per + p] = k
                vcur[side * per + p] = kvx[g, side, 1, p]
                ktb[side * per + p] = k.T

        sides = {}
        tops = {}

        def products(i):
            q = qin[g, i] * jnp.bfloat16(0.125)
            do = doin[g, i]
            zero = jnp.zeros_like(q)
            qd = jnp.concatenate([jnp.where(lane_low, q, zero), jnp.where(lane_low, zero, q)], 0)
            dd = jnp.concatenate([jnp.where(lane_low, do, zero), jnp.where(lane_low, zero, do)], 0)
            qb[i % 3][...] = qd
            dob[i % 3][...] = dd
            ids = [lid[i, j] for j in range(listed)]
            s = nt(jnp.concatenate([kcur[t] for t in ids], 0), qd)
            top = None
            for j in range(listed):
                low, high = j * PATCH, j * PATCH + PATCH // 2
                s_low = s[low:high]
                s_high = jnp.where(half_row < ecnt[ids[j]], s[high : low + PATCH], -jnp.inf)
                sb[i % 2][low:high] = s_low
                sb[i % 2][high : low + PATCH] = s_high
                for part in (s_low, s_high):
                    part = jnp.max(part.reshape(-1, 8, 2 * PATCH), axis=0)
                    top = part if top is None else jnp.maximum(top, part)
            tops[i] = jnp.max(top, axis=0, keepdims=True)
            dpb[i % 2][...] = nt(jnp.concatenate([vcur[t] for t in ids], 0), dd)

        def middle(i):
            scores, grads = sb[i % 2], dpb[i % 2]
            top = tops[i]
            step = PATCH // 2
            total_e = total_d = None
            for low in range(0, listed * PATCH, step):
                e = jnp.exp(scores[low : low + step] - top)
                scores[low : low + step] = e
                d = e * grads[low : low + step]
                e = jnp.sum(e.reshape(-1, 8, 2 * PATCH), axis=0)
                d = jnp.sum(d.reshape(-1, 8, 2 * PATCH), axis=0)
                total_e = e if total_e is None else total_e + e
                total_d = d if total_d is None else total_d + d
            inverse = 1.0 / jnp.sum(total_e, axis=0, keepdims=True)
            delta = jnp.sum(total_d, axis=0, keepdims=True) * inverse
            for low in range(0, listed * PATCH, step):
                a = scores[low : low + step] * inverse
                pb[i % 2][low : low + step] = a.astype(jnp.bfloat16)
                dsb[i % 2][low : low + step] = (a * (grads[low : low + step] - delta)).astype(
                    jnp.bfloat16
                )

        def results(i):
            ds = dsb[i % 2][...]
            kt = jnp.concatenate([ktb[lid[i, j]] for j in range(listed)], 1)
            dq = nn(kt, ds)
            dq = jnp.where(row_low, dq[:, :PATCH], dq[:, PATCH:])
            dqs[g, i] = (dq.T * 0.125).astype(jnp.bfloat16)
            dk = nn(ds, qb[i % 3][...])
            dv = nn(pb[i % 2][...], dob[i % 3][...])
            for j in range(listed):
                ck[i, j] = dk[j * PATCH : (j + 1) * PATCH]
                cv[i, j] = dv[j * PATCH : (j + 1) * PATCH]

        for n in range(per + 2):
            if n >= 2:
                results(n - 2)
            if n < per:
                products(n)
            if 1 <= n <= per:
                middle(n - 1)

        out(0, g).start()

        for t in list(range(per)) + list(range(2 * per, ext)) + list(range(per, 2 * per)):
            first, last = max(0, t - 2 * per), min(per - 1, t)
            slots = [inv[i, t - i] for i in range(first, last + 1)]
            for kind, terms in ((0, ck), (1, cv)):
                value = functools.reduce(
                    jnp.add, [terms[i, slot] for i, slot in zip(range(first, last + 1), slots)]
                )
                if t < per:
                    gsend[g, 0, kind, t] = value.astype(jnp.bfloat16)
                elif t >= 2 * per:
                    gsend[g, 1, kind, t - 2 * per] = value.astype(jnp.bfloat16)
                else:
                    own[g, kind, t - per] = value
        for which in range(2):
            gr_send(which, g).start()

        @pl.when(g >= LAG)
        def _():
            finish(g - LAG)

    @pl.loop(groups - LAG, groups)
    def _(g):
        finish(g)

    @pl.loop(0, groups)
    def _(g):
        for which in range(2):
            kv_send(which, g).wait_send()
            gr_send(which, g).wait_send()
        for which in range(3):
            out(which, g).wait()


def pass_on(a_ref, b_ref, c_ref, x_ref, y_ref, z_ref):
    x_ref[...] = a_ref[...]
    y_ref[...] = b_ref[...]
    z_ref[...] = c_ref[...]


def on_device(queries, keys, values, grad_out, pattern, counts):
    rows, width = queries.shape
    per = rows // PATCH
    total, listed = pattern.shape
    devices = lax.axis_size("space")
    groups = width // LANES
    ext = 3 * per
    shape = jax.ShapeDtypeStruct((per, PATCH, width), jnp.bfloat16)
    low = jnp.bfloat16
    full = jnp.float32
    anywhere = pl.BlockSpec(memory_space=pl.ANY)
    small = pl.BlockSpec(memory_space=pltpu.SMEM)
    outs = pl.pallas_call(
        functools.partial(kernel, devices, per, listed, total),
        out_shape=(shape,) * 3,
        in_specs=[small, small] + [anywhere] * 4,
        out_specs=[anywhere] * 3,
        scratch_shapes=[
            pltpu.VMEM((groups, 3, 2, per, PATCH, LANES), low),
            pltpu.VMEM((groups, per, PATCH, LANES), low),
            pltpu.VMEM((groups, per, PATCH, LANES), low),
            pltpu.VMEM((ext, PATCH, LANES), low),
            pltpu.VMEM((ext, PATCH, LANES), low),
            pltpu.VMEM((ext, LANES, PATCH), low),
            [pltpu.VMEM((2 * PATCH, LANES), low)] * 3,
            [pltpu.VMEM((2 * PATCH, LANES), low)] * 3,
            [pltpu.VMEM((listed * PATCH, 2 * PATCH), full)] * 2,
            [pltpu.VMEM((listed * PATCH, 2 * PATCH), full)] * 2,
            [pltpu.VMEM((listed * PATCH, 2 * PATCH), low)] * 2,
            [pltpu.VMEM((listed * PATCH, 2 * PATCH), low)] * 2,
            pltpu.VMEM((per, listed + 1, PATCH, LANES), full),
            pltpu.VMEM((per, listed + 1, PATCH, LANES), full),
            pltpu.VMEM((groups, 2, 2, per, PATCH, LANES), low),
            pltpu.VMEM((groups, 2, 2, per, PATCH, LANES), low),
            pltpu.VMEM((groups, 2, per, PATCH, LANES), full),
            pltpu.VMEM((groups, per, PATCH, LANES), low),
            pltpu.VMEM((groups, per, PATCH, LANES), low),
            pltpu.VMEM((groups, per, PATCH, LANES), low),
            pltpu.SMEM((per, listed), jnp.int32),
            pltpu.SMEM((per, 2 * per + 1), jnp.int32),
            pltpu.SMEM((ext,), jnp.int32),
            pltpu.SemaphoreType.DMA((4, groups)),
            pltpu.SemaphoreType.DMA((2, groups)),
            pltpu.SemaphoreType.DMA((2, groups)),
            pltpu.SemaphoreType.DMA((2, groups)),
            pltpu.SemaphoreType.DMA((2, groups)),
            pltpu.SemaphoreType.DMA((3, groups)),
        ],
        compiler_params=pltpu.CompilerParams(
            collective_id=0, has_side_effects=True, vmem_limit_bytes=60 * 1024 * 1024
        ),
        name="sparse_attention_backward",
    )(pattern.T, counts, *(x.reshape(per, PATCH, width) for x in (queries, keys, values, grad_out)))
    block = pl.BlockSpec((rows // STEPS, width), lambda i: (i, 0))
    return pl.pallas_call(
        pass_on,
        out_shape=(jax.ShapeDtypeStruct((rows, width), low),) * 3,
        grid=(STEPS,),
        in_specs=[block] * 3,
        out_specs=[block] * 3,
        name="pass_on",
    )(*(x.reshape(rows, width) for x in outs))


def solution(mesh):
    rows = P(("scene", "space"), None)
    return jax.shard_map(
        on_device,
        mesh=mesh,
        in_specs=(rows, rows, rows, rows, P("scene", None), P("scene")),
        out_specs=(rows, rows, rows),
        check_vma=False,
    )
```
